256 devices in a mesh: rows: 16 (over y, x), keys: 16 (over z, core).
Axes of the slice: x: 4, y: 4, z: 8, core: 2. Of those that a mesh axis runs over, the one named last changes fastest.
Arguments:
- pair_rep: bfloat16 [768, 768, 128], P('rows', 'keys'), may hold values from -6 to 6
- norm_gain: float32 [128], replicated, may hold values from 0.1 to 1.9
- w_query: bfloat16 [128, 128], replicated, may hold values from -0.5 to 0.5
- w_key: bfloat16 [128, 128], replicated, may hold values from -0.5 to 0.5
- w_value: bfloat16 [128, 128], replicated, may hold values from -0.5 to 0.5
- w_gate: bfloat16 [128, 128], replicated, may hold values from -0.5 to 0.5
- w_out: bfloat16 [128, 128], replicated, may hold values from -0.5 to 0.5
- pair_bias: bfloat16 [4, 768, 768], P(None, 'keys', 'rows'), may hold values from -12 to 300
Outputs:
- update: bfloat16 [768, 768, 128], P('rows', 'keys')
The draws below stay inside these ranges and needn't reach their ends.
All inputs are finite; a program needn't handle non-finite values.
Results may differ from the reference program's by a relative error of at most 0.025.
Values may be sent and summed in bfloat16 or wider, within the bound.
A program may use at most 128 MiB of HBM per device.

```python
import jax
import jax.numpy as jnp
from jax import lax

CHANNELS = 128
HEADS = 4
HEAD_SIZE = 32
ROWS = 768
LENGTH = 768


def draw_pair_bias(key, part):
    shape = (HEADS, LENGTH, LENGTH)
    result = jnp.clip(2.0 * jax.random.normal(jax.random.fold_in(key, 6), shape, jnp.float32), -12.0, 12.0)
    return result.astype(jnp.bfloat16)


def block_scale(own_key, dims, split, low, high):
    level = 1.0
    for position, parts in split:
        draws = jax.random.uniform(jax.random.fold_in(jax.random.fold_in(own_key, 6), position), (parts,), jnp.float32, low / len(split), high / len(split))
        level = level * jnp.repeat(jnp.exp(draws), dims[position] // parts).reshape((-1,) + (1,) * (len(dims) - 1 - position))
    return level


def centred(stream_key, dims, deviation, limit, shards=(), held_as=jnp.bfloat16):
    factor_of = block_scale(stream_key, dims, shards, -0.22, 0.18) if shards else 1.0
    array = jax.random.normal(stream_key, dims, jnp.float32) * deviation * factor_of
    return jnp.minimum(jnp.maximum(array, -limit), limit).astype(held_as)


def setup_inputs(seed: int = 0) -> dict:
    splits = jax.random.split(jax.random.key(seed), 9)
    return {
        "pair_rep": centred(splits[0], (ROWS, LENGTH, CHANNELS), 1.0, 6.0, ((0, 16), (1, 16))),
        "norm_gain": jnp.clip(1.0 + 0.18 * jax.random.normal(splits[1], (CHANNELS,), jnp.float32), 0.1, 1.9),
        "w_query": centred(splits[2], (CHANNELS, HEADS * HEAD_SIZE), CHANNELS ** -0.5, 0.5),
        "w_key": centred(splits[3], (CHANNELS, HEADS * HEAD_SIZE), CHANNELS ** -0.5, 0.5),
        "w_value": centred(splits[4], (CHANNELS, HEADS * HEAD_SIZE), CHANNELS ** -0.5, 0.5),
        "w_gate": centred(splits[5], (CHANNELS, HEADS * HEAD_SIZE), CHANNELS ** -0.5, 0.5),
        "w_out": centred(splits[6], (HEADS * HEAD_SIZE, CHANNELS), (HEADS * HEAD_SIZE) ** -0.5, 0.5),
        "pair_bias": draw_pair_bias(jax.random.fold_in(splits[8], 71), 0),
    }


epsilon = 1e-05

def normalize(pair_rep, norm_gain):
    values = pair_rep.astype(jnp.float32)
    center = lax.optimization_barrier(jnp.mean(values, axis=-1, keepdims=True))
    spread = lax.optimization_barrier(jnp.mean(jnp.square(values - center), axis=-1, keepdims=True))
    return ((values - center) * lax.rsqrt(spread + epsilon) * norm_gain).astype(jnp.bfloat16)

def split_heads(tensor, head_count):
    return tensor.reshape(tensor.shape[:-1] + (head_count, tensor.shape[-1] // head_count))

def reference(pair_rep, norm_gain, w_query, w_key, w_value, w_gate, w_out, pair_bias):
    head_count = pair_bias.shape[0]
    inner_width = w_query.shape[1]
    normed = normalize(pair_rep, norm_gain)
    queries = (jnp.dot(normed, w_query, preferred_element_type=jnp.float32) * (inner_width // head_count) ** (-0.5)).astype(jnp.bfloat16)
    key_rows = jnp.dot(normed, w_key, preferred_element_type=jnp.float32).astype(jnp.bfloat16)
    value_rows = jnp.dot(normed, w_value, preferred_element_type=jnp.float32).astype(jnp.bfloat16)
    gates = jax.nn.sigmoid(jnp.dot(normed, w_gate, preferred_element_type=jnp.float32))
    bias_values = pair_bias.astype(jnp.float32)

    def one_row(arrays):
        query_row, key_row, value_row = arrays
        logits = jnp.einsum('jhd,khd->hjk', split_heads(query_row.astype(jnp.float32), head_count), split_heads(key_row.astype(jnp.float32), head_count), precision=lax.Precision.HIGHEST) + bias_values
        highest = lax.optimization_barrier(jnp.max(logits, axis=2, keepdims=True))
        powers = jnp.exp(logits - highest)
        totals = lax.optimization_barrier(jnp.sum(powers, axis=2))
        weights = lax.optimization_barrier(powers.astype(jnp.bfloat16)).astype(jnp.float32)
        summed = jnp.einsum('hjk,khd->jhd', weights, split_heads(value_row.astype(jnp.float32), head_count), precision=lax.Precision.HIGHEST)
        return (summed / jnp.transpose(totals)[..., None]).reshape(query_row.shape[0], inner_width)
    attended = lax.map(one_row, (queries, key_rows, value_rows))
    gated = (gates * attended).astype(jnp.bfloat16)
    return jnp.dot(gated, w_out, preferred_element_type=jnp.float32).astype(jnp.bfloat16)
```

```python
import functools
import math

import jax
import jax.numpy as jnp
from jax import lax
from jax.experimental import pallas as pl
from jax.experimental.pallas import tpu as pltpu
from jax.sharding import Mesh
from jax.sharding import PartitionSpec as P

AXES = ("y", "x", "z", "c")
MESH = pl.DeviceIdType.MESH
BF16, F32 = jnp.bfloat16, jnp.float32
NY, NX, NZ, NC = 4, 4, 8, 2
HEADS, DIM, CH = 4, 32, 128
BLK = 48
OWN = BLK // NZ
QRY = NZ * BLK
KEYS = NC * QRY
LANES = 128
CHUNKS = QRY // LANES
EPS = 1e-05
LOG2E = math.log2(math.e)
Z_ORDER = (4, 3, 5, 2, 6, 1, 7)
NT = (((1,), (1,)), ((), ()))
DONE = ((0, 1), (2, 3, 4), (5, 6, 7))


def dot(a, b):
    return jnp.dot(a, b, preferred_element_type=F32)


def dot_nt(a, b):
    return lax.dot_general(a, b, NT, preferred_element_type=F32)


def kernel(
    x_hbm, gain, w_query, w_key, w_value, w_gate, w_out, pair_bias, out_hbm,
    xbuf, zbias, bias, bias32, keys, values, queries, gates, wq_t, wv_t, wg_t, outbuf,
    zs, zr, as_, ar, bs, br, xs, xr, xl, fs, fr, os_, or_, ol,
):
    y, x, z, c = (lax.axis_index(a) for a in AXES)
    at = {"x": x, "y": y}

    def remote(src, dst, send, recv, **where):
        return pltpu.make_async_remote_copy(
            src_ref=src, dst_ref=dst, send_sem=send, recv_sem=recv, device_id=where, device_id_type=MESH
        )

    def wait(ref, sem):
        pltpu.make_async_copy(ref, ref, sem).wait()

    barrier = pltpu.get_barrier_semaphore()
    peers = [{"z": lax.rem(z + k, NZ)} for k in range(1, NZ)]
    peers += [{a: lax.rem(at[a] + k, 4)} for a in "xy" for k in range(1, 4)]
    peers += [{"c": 1 - c}]
    for peer in peers:
        pl.semaphore_signal(barrier, inc=1, device_id=peer, device_id_type=MESH)

    own_rows = pltpu.make_async_copy(x_hbm.at[pl.ds(z * OWN, OWN)], xbuf.at[:, 0, z], xl)
    own_rows.start()

    for g in range(2):
        packed = jnp.zeros((BLK, LANES), F32)
        for hh in range(2):
            row = lax.broadcasted_iota(jnp.int32, (BLK, LANES), 0)
            lane = lax.broadcasted_iota(jnp.int32, (BLK, LANES), 1)
            place = jnp.where(lane == row + BLK * hh, 1.0, 0.0).astype(BF16)
            packed = packed + dot(pair_bias[2 * g + hh], place)
        zbias[z, g] = packed.astype(BF16)
    for src, dst in ((w_query, wq_t), (w_value, wv_t), (w_gate, wg_t)):
        dst[...] = jnp.transpose(src[...].astype(F32)).astype(BF16)
    values[:, :, 2 * DIM :, :] = jnp.ones((OWN, 2, 16, KEYS), BF16)

    pl.semaphore_wait(barrier, len(peers))

    for k in Z_ORDER:
        remote(zbias.at[z], zbias.at[z], zs, zr, z=lax.rem(z + k, NZ)).start()

    def send_row(i, _):
        for k in Z_ORDER:
            t = lax.rem(z + k, NZ)
            remote(x_hbm.at[t * OWN + i], xbuf.at[i, 0, z], xs, xr.at[i], z=t).start()
        return 0

    lax.fori_loop(0, OWN, send_row, 0)

    wait(zbias.at[pl.ds(0, NZ - 1)], zr)
    o = jnp.where(lax.rem(x, 2) == c, 0, 1)
    x2 = x // 2
    for g in range(2):
        block = zbias[:, g].reshape(QRY, LANES)
        for hh in range(2):
            row = lax.broadcasted_iota(jnp.int32, (BLK, LANES), 0)
            lane = lax.broadcasted_iota(jnp.int32, (BLK, LANES), 1)
            place = jnp.where(lane == row + BLK * hh, 1.0, 0.0).astype(BF16)
            part = dot_nt(place, block).astype(BF16)
            for t in range(CHUNKS):
                bias[t, 2 * g + hh, o, y, x2] = part[:, LANES * t : LANES * (t + 1)]
    for t in range(CHUNKS):
        for half, axis in ((0, "x"), (1, "y")):
            mine = bias.at[t, pl.ds(2 * half, 2), o, y, x2]
            for k in (2, 1, 3):
                there = lax.rem(at[axis] + k, 4)
                remote(mine, mine, as_, ar.at[t, half], **{axis: there}).start()
    for t in range(CHUNKS):
        for half, axis in ((0, "y"), (1, "x")):
            wait(bias.at[t, pl.ds(0, 2), 0, pl.ds(0, 3), 0], ar.at[t, half])
            if half == 0:
                line = bias.at[t, pl.ds(0, 2), :, y]
            else:
                line = bias.at[t, pl.ds(2, 2), o, :, x2]
            for k in (2, 1, 3):
                there = lax.rem(at[axis] + k, 4)
                remote(line, line, bs, br.at[t, half], **{axis: there}).start()

    def normed(i, side):
        v = xbuf[i, side].reshape(QRY, CH).astype(F32)
        v = v - jnp.mean(v, axis=-1, keepdims=True)
        spread = jnp.mean(jnp.square(v), axis=-1, keepdims=True)
        return (v * lax.rsqrt(spread + EPS) * gain[...]).astype(BF16)

    def project(i, side, n):
        cols = pl.ds(side * QRY, QRY)
        keys[i, cols, :] = dot(n, w_key[...]).astype(BF16)
        v = dot_nt(wv_t[...], n).astype(BF16)
        values[i, 0, : 2 * DIM, cols] = v[: 2 * DIM]
        values[i, 1, : 2 * DIM, cols] = v[2 * DIM :]

    own_rows.wait()

    def own_side(i, _):
        wait(xbuf.at[i, 0, pl.ds(0, NZ - 1)], xr.at[i])
        remote(xbuf.at[i, 0], xbuf.at[i, 1], fs, fr.at[i], c=1 - c).start()
        n = normed(i, 0)
        project(i, 0, n)
        queries[i] = (dot_nt(wq_t[...], n) * (DIM**-0.5 * LOG2E)).astype(BF16)
        gates[i] = jax.nn.sigmoid(dot_nt(wg_t[...], n))
        return 0

    lax.fori_loop(0, OWN, own_side, 0)

    def other_side(i, _):
        wait(xbuf.at[i, 1], fr.at[i])
        project(i, 1, normed(i, 1))
        return 0

    lax.fori_loop(0, OWN, other_side, 0)

    for t in range(CHUNKS):
        lanes = slice(LANES * t, LANES * (t + 1))
        for half in range(2):
            wait(bias.at[t, pl.ds(0, 2), :, pl.ds(0, 3)], br.at[t, half])
        for h in range(HEADS):
            bias32[h // 2, :, LANES * (h % 2) : LANES * (h % 2 + 1)] = (
                bias[t, h].reshape(KEYS, LANES).astype(F32) * LOG2E
            )

        def attend(i, _):
            q = queries[i, :, lanes]
            head = lax.broadcasted_iota(jnp.int32, (CH, LANES), 0) // DIM
            rows = []
            for g in range(2):
                zero = jnp.zeros_like(q)
                rhs = jnp.concatenate([jnp.where(head == 2 * g + hh, q, zero) for hh in range(2)], axis=1)
                s = dot(keys[i], rhs) + bias32[g]
                p = jnp.exp2(s - jnp.max(s, axis=0, keepdims=True)).astype(BF16)
                sums = dot(values[i, g], p)
                for hh in range(2):
                    side = slice(LANES * hh, LANES * (hh + 1))
                    rows.append(sums[DIM * hh : DIM * (hh + 1), side] / sums[2 * DIM : 2 * DIM + 1, side])
            gated = jnp.concatenate(rows, axis=0) * gates[i, :, lanes]
            gated = jnp.transpose(gated).astype(BF16)
            outbuf[i, lanes, :] = dot(gated, w_out[...]).astype(BF16)
            for b in DONE[t]:
                done = outbuf.at[i, pl.ds(BLK * b, BLK)]

                @pl.when(z != b)
                def _():
                    remote(done, out_hbm.at[z * OWN + i], os_, or_, z=b).start()

                @pl.when(z == b)
                def _():
                    pltpu.make_async_copy(done, out_hbm.at[z * OWN + i], ol).start()

            return 0

        lax.fori_loop(0, OWN, attend, 0)

    wait(out_hbm.at[pl.ds(0, OWN * (NZ - 1))], or_)
    wait(out_hbm.at[pl.ds(0, OWN * (NZ - 1))], os_)
    wait(out_hbm.at[pl.ds(0, OWN)], ol)
    wait(zbias.at[pl.ds(0, NZ - 1)], zs)
    wait(x_hbm.at[pl.ds(0, OWN * (NZ - 1))], xs)
    wait(xbuf.at[:, 0], fs)
    for t in range(CHUNKS):
        for half in range(2):
            wait(bias.at[t, pl.ds(0, 2), 0, pl.ds(0, 3), 0], as_)
            wait(bias.at[t, pl.ds(0, 2), :, pl.ds(0, 3)], bs)


def body(pair_rep, norm_gain, w_query, w_key, w_value, w_gate, w_out, pair_bias):
    vmem = pl.BlockSpec(memory_space=pltpu.VMEM)
    anywhere = pl.BlockSpec(memory_space=pl.ANY)
    dma = pltpu.SemaphoreType.DMA
    return pl.pallas_call(
        kernel,
        out_shape=jax.ShapeDtypeStruct((BLK, BLK, CH), BF16),
        in_specs=[anywhere] + [vmem] * 7,
        out_specs=anywhere,
        scratch_shapes=[
            pltpu.VMEM((OWN, 2, NZ, BLK, CH), BF16),
            pltpu.VMEM((NZ, 2, BLK, LANES), BF16),
            pltpu.VMEM((CHUNKS, HEADS, 2, NY, NX // 2, BLK, LANES), BF16),
            pltpu.VMEM((2, KEYS, 2 * LANES), F32),
            pltpu.VMEM((OWN, KEYS, CH), BF16),
            pltpu.VMEM((OWN, 2, 2 * DIM + 16, KEYS), BF16),
            pltpu.VMEM((OWN, CH, QRY), BF16),
            pltpu.VMEM((OWN, CH, QRY), F32),
            pltpu.VMEM((CH, CH), BF16),
            pltpu.VMEM((CH, CH), BF16),
            pltpu.VMEM((CH, CH), BF16),
            pltpu.VMEM((OWN, QRY, CH), BF16),
            dma, dma,
            dma, dma((CHUNKS, 2)),
            dma, dma((CHUNKS, 2)),
            dma, dma((OWN,)), dma,
            dma, dma((OWN,)),
            dma, dma, dma,
        ],
        compiler_params=pltpu.CompilerParams(
            collective_id=0, has_side_effects=True, vmem_limit_bytes=56 * 1024 * 1024
        ),
        name="triangle_attention",
    )(pair_rep, norm_gain.reshape(1, CH), w_query, w_key, w_value, w_gate, w_out, pair_bias)


def solution(mesh):
    torus = Mesh(mesh.devices.reshape(NY, NX, NZ, NC), AXES)
    rows, cols = ("y", "x"), ("z", "c")
    placed = (P(rows, cols, None), P(), P(), P(), P(), P(), P(), P(None, cols, rows))
    return jax.shard_map(body, mesh=torus, in_specs=placed, out_specs=P(rows, cols, None), check_vma=False)
```

```python
import functools
import math

import jax
import jax.numpy as jnp
from jax import lax
from jax.experimental import pallas as pl
from jax.experimental.pallas import tpu as pltpu
from jax.sharding import Mesh
from jax.sharding import PartitionSpec as P

AXES = ("y", "x", "z", "c")
MESH = pl.DeviceIdType.MESH
BF16, F32 = jnp.bfloat16, jnp.float32
NY, NX, NZ, NC = 4, 4, 8, 2
HEADS, DIM, CH = 4, 32, 128
BLK = 48
OWN = BLK // NZ
QRY = NZ * BLK
KEYS = NC * QRY
LANES = 128
CHUNKS = QRY // LANES
EPS = 1e-05
STEP = 128
LOG2E = math.log2(math.e)
Z_ORDER = (4, 3, 5, 2, 6, 1, 7)
NT = (((1,), (1,)), ((), ()))
OFFSETS = (3, 5, 4, 2, 6, 1, 7, 0)
PLACE = tuple(OFFSETS.index(d) for d in range(8))
DONE = ((0, 1), (2, 3, 4), (5, 6, 7))


def dot(a, b):
    return jnp.dot(a, b, preferred_element_type=F32)


def dot_nt(a, b):
    return lax.dot_general(a, b, NT, preferred_element_type=F32)


def kernel(
    x_hbm, gain, w_query, w_key, w_value, w_gate, w_out, pair_bias, out_hbm,
    xbuf, zbias, bias, bias32, keys, values, queries, gates, wq_t, wv_t, wg_t, outbuf, s0, s1, top0, top1,
    zs, zr, as_, ar, bs, br, xs, xr, xl, fs, fr, os_, or_, ol,
):
    y, x, z, c = (lax.axis_index(a) for a in AXES)
    at = {"x": x, "y": y}

    def remote(src, dst, send, recv, **where):
        return pltpu.make_async_remote_copy(
            src_ref=src, dst_ref=dst, send_sem=send, recv_sem=recv, device_id=where, device_id_type=MESH
        )

    def wait(ref, sem):
        pltpu.make_async_copy(ref, ref, sem).wait()

    barrier = pltpu.get_barrier_semaphore()
    peers = [{"z": lax.rem(z + k, NZ)} for k in range(1, NZ)]
    peers += [{a: lax.rem(at[a] + k, 4)} for a in "xy" for k in range(1, 4)]
    peers += [{"c": 1 - c}]
    for peer in peers:
        pl.semaphore_signal(barrier, inc=1, device_id=peer, device_id_type=MESH)

    own_rows = pltpu.make_async_copy(x_hbm.at[pl.ds(z * OWN, OWN)], xbuf.at[:, 0, PLACE[0]], xl)
    own_rows.start()

    for g in range(2):
        packed = jnp.zeros((BLK, LANES), F32)
        for hh in range(2):
            row = lax.broadcasted_iota(jnp.int32, (BLK, LANES), 0)
            lane = lax.broadcasted_iota(jnp.int32, (BLK, LANES), 1)
            place = jnp.where(lane == row + BLK * hh, 1.0, 0.0).astype(BF16)
            packed = packed + dot(pair_bias[2 * g + hh], place)
        zbias[PLACE[0], g] = packed.astype(BF16)
    for src, dst in ((w_query, wq_t), (w_value, wv_t), (w_gate, wg_t)):
        dst[...] = jnp.transpose(src[...].astype(F32)).astype(BF16)
    values[:, :, 2 * DIM :, :] = jnp.ones((OWN, 2, 16, KEYS), BF16)

    pl.semaphore_wait(barrier, len(peers))

    for k in Z_ORDER:
        remote(zbias.at[PLACE[0]], zbias.at[PLACE[NZ - k]], zs, zr, z=lax.rem(z + k, NZ)).start()

    def send_row(i, _):
        for k in Z_ORDER:
            t = lax.rem(z + k, NZ)
            remote(x_hbm.at[t * OWN + i], xbuf.at[i, 0, PLACE[NZ - k]], xs, xr.at[i], z=t).start()
        return 0

    lax.fori_loop(0, OWN, send_row, 0)

    wait(zbias.at[pl.ds(0, NZ - 1)], zr)
    o = jnp.where(lax.rem(x, 2) == c, 0, 1)
    x2 = x // 2
    for g in range(2):
        block = zbias[:, g].reshape(QRY, LANES)
        for hh in range(2):
            row = lax.broadcasted_iota(jnp.int32, (BLK, LANES), 0)
            lane = lax.broadcasted_iota(jnp.int32, (BLK, LANES), 1)
            place = jnp.where(lane == row + BLK * hh, 1.0, 0.0).astype(BF16)
            part = dot_nt(place, block).astype(BF16)
            for t in range(CHUNKS):
                bias[t, 2 * g + hh, o, y, x2] = part[:, LANES * t : LANES * (t + 1)]
    for t in range(CHUNKS):
        for half, axis in ((0, "x"), (1, "y")):
            mine = bias.at[t, pl.ds(2 * half, 2), o, y, x2]
            for k in (2, 1, 3):
                there = lax.rem(at[axis] + k, 4)
                remote(mine, mine, as_, ar.at[t, half], **{axis: there}).start()
    for t in range(CHUNKS):
        for half, axis in ((0, "y"), (1, "x")):
            wait(bias.at[t, pl.ds(0, 2), 0, pl.ds(0, 3), 0], ar.at[t, half])
            if half == 0:
                line = bias.at[t, pl.ds(0, 2), :, y]
            else:
                line = bias.at[t, pl.ds(2, 2), o, :, x2]
            for k in (2, 1, 3):
                there = lax.rem(at[axis] + k, 4)
                remote(line, line, bs, br.at[t, half], **{axis: there}).start()

    def normed(i, side):
        v = xbuf[i, side].reshape(QRY, CH).astype(F32)
        v = v - jnp.mean(v, axis=-1, keepdims=True)
        spread = jnp.mean(jnp.square(v), axis=-1, keepdims=True)
        return (v * lax.rsqrt(spread + EPS) * gain[...]).astype(BF16)

    def project(i, side, n):
        cols = pl.ds(side * QRY, QRY)
        keys[i, cols, :] = dot(n, w_key[...]).astype(BF16)
        v = dot_nt(wv_t[...], n).astype(BF16)
        values[i, 0, : 2 * DIM, cols] = v[: 2 * DIM]
        values[i, 1, : 2 * DIM, cols] = v[2 * DIM :]

    own_rows.wait()

    def own_side(i, _):
        wait(xbuf.at[i, 0, pl.ds(0, NZ - 1)], xr.at[i])
        remote(xbuf.at[i, 0], xbuf.at[i, 1], fs, fr.at[i], c=1 - c).start()
        n = normed(i, 0)
        project(i, 0, n)
        queries[i] = (dot_nt(wq_t[...], n) * (DIM**-0.5 * LOG2E)).astype(BF16)
        gates[i] = jax.nn.sigmoid(dot_nt(wg_t[...], n))
        return 0

    lax.fori_loop(0, OWN, own_side, 0)

    def other_side(i, _):
        wait(xbuf.at[i, 1], fr.at[i])
        project(i, 1, normed(i, 1))
        return 0

    lax.fori_loop(0, OWN, other_side, 0)

    place = []
    for b in range(NZ):
        away = lax.rem(b - z + NZ, NZ)
        place.append(sum(jnp.where(away == d, PLACE[d], 0) for d in range(NZ)))

    for t in range(CHUNKS):
        lanes = slice(LANES * t, LANES * (t + 1))
        for half in range(2):
            wait(bias.at[t, pl.ds(0, 2), :, pl.ds(0, 3)], br.at[t, half])
        for h in range(HEADS):
            for side in range(2):
                for b in range(NZ):
                    rows = pl.ds(pl.multiple_of(side * QRY + BLK * place[b], 16), BLK)
                    bias32[h // 2, rows, LANES * (h % 2) : LANES * (h % 2 + 1)] = (
                        bias[t, h, side, b // 2, b % 2].astype(F32) * LOG2E
                    )

        def scores(i, g, s_ref, top_ref):
            q = queries[i, :, lanes]
            head = lax.broadcasted_iota(jnp.int32, (CH, LANES), 0) // DIM
            rhs = jnp.concatenate([jnp.where(head == 2 * g + hh, q, jnp.zeros_like(q)) for hh in range(2)], axis=1)
            top = None
            for k in range(0, KEYS, STEP):
                s = dot(keys[i, k : k + STEP, :], rhs) + bias32[g, k : k + STEP, :]
                s_ref[k : k + STEP, :] = s
                peak = jnp.max(s.reshape(STEP // 8, 8, 2 * LANES), axis=0)
                top = peak if top is None else jnp.maximum(top, peak)
            top_ref[...] = top

        def weigh(i, g, s_ref, top_ref):
            top = jnp.max(top_ref[...], axis=0, keepdims=True)
            p = [jnp.exp2(s_ref[k : k + STEP, :] - top).astype(BF16) for k in range(0, KEYS, STEP)]
            sums = dot(values[i, g], jnp.concatenate(p, axis=0))
            rows = []
            for hh in range(2):
                side = slice(LANES * hh, LANES * (hh + 1))
                rows.append(sums[DIM * hh : DIM * (hh + 1), side] / sums[2 * DIM : 2 * DIM + 1, side])
            return jnp.concatenate(rows, axis=0)

        scores(0, 0, s0, top0)

        def attend(i, _):
            scores(i, 1, s1, top1)
            first = weigh(i, 0, s0, top0)
            scores(jnp.minimum(i + 1, OWN - 1), 0, s0, top0)
            second = weigh(i, 1, s1, top1)
            gated = jnp.concatenate([first, second], axis=0) * gates[i, :, lanes]
            gated = jnp.transpose(gated).astype(BF16)
            outbuf[i, lanes, :] = dot(gated, w_out[...]).astype(BF16)
            for b in DONE[t]:
                done, there = outbuf.at[i, pl.ds(BLK * b, BLK)], out_hbm.at[z * OWN + i]
                if OFFSETS[b]:
                    remote(done, there, os_, or_, z=lax.rem(z + OFFSETS[b], NZ)).start()
                else:
                    pltpu.make_async_copy(done, there, ol).start()
            return 0

        lax.fori_loop(0, OWN, attend, 0)

    wait(out_hbm.at[pl.ds(0, OWN * (NZ - 1))], or_)
    wait(out_hbm.at[pl.ds(0, OWN * (NZ - 1))], os_)
    wait(out_hbm.at[pl.ds(0, OWN)], ol)
    wait(zbias.at[pl.ds(0, NZ - 1)], zs)
    wait(x_hbm.at[pl.ds(0, OWN * (NZ - 1))], xs)
    wait(xbuf.at[:, 0], fs)
    for t in range(CHUNKS):
        for half in range(2):
            wait(bias.at[t, pl.ds(0, 2), 0, pl.ds(0, 3), 0], as_)
            wait(bias.at[t, pl.ds(0, 2), :, pl.ds(0, 3)], bs)


def body(pair_rep, norm_gain, w_query, w_key, w_value, w_gate, w_out, pair_bias):
    vmem = pl.BlockSpec(memory_space=pltpu.VMEM)
    anywhere = pl.BlockSpec(memory_space=pl.ANY)
    dma = pltpu.SemaphoreType.DMA
    return pl.pallas_call(
        kernel,
        out_shape=jax.ShapeDtypeStruct((BLK, BLK, CH), BF16),
        in_specs=[anywhere] + [vmem] * 7,
        out_specs=anywhere,
        scratch_shapes=[
            pltpu.VMEM((OWN, 2, NZ, BLK, CH), BF16),
            pltpu.VMEM((NZ, 2, BLK, LANES), BF16),
            pltpu.VMEM((CHUNKS, HEADS, 2, NY, NX // 2, BLK, LANES), BF16),
            pltpu.VMEM((2, KEYS, 2 * LANES), F32),
            pltpu.VMEM((OWN, KEYS, CH), BF16),
            pltpu.VMEM((OWN, 2, 2 * DIM + 16, KEYS), BF16),
            pltpu.VMEM((OWN, CH, QRY), BF16),
            pltpu.VMEM((OWN, CH, QRY), F32),
            pltpu.VMEM((CH, CH), BF16),
            pltpu.VMEM((CH, CH), BF16),
            pltpu.VMEM((CH, CH), BF16),
            pltpu.VMEM((OWN, QRY, CH), BF16),
            pltpu.VMEM((KEYS, 2 * LANES), F32),
            pltpu.VMEM((KEYS, 2 * LANES), F32),
            pltpu.VMEM((8, 2 * LANES), F32),
            pltpu.VMEM((8, 2 * LANES), F32),
            dma, dma,
            dma, dma((CHUNKS, 2)),
            dma, dma((CHUNKS, 2)),
            dma, dma((OWN,)), dma,
            dma, dma((OWN,)),
            dma, dma, dma,
        ],
        compiler_params=pltpu.CompilerParams(
            collective_id=0, has_side_effects=True, vmem_limit_bytes=56 * 1024 * 1024
        ),
        name="triangle_attention",
    )(pair_rep, norm_gain.reshape(1, CH), w_query, w_key, w_value, w_gate, w_out, pair_bias)


def solution(mesh):
    torus = Mesh(mesh.devices.reshape(NY, NX, NZ, NC), AXES)
    rows, cols = ("y", "x"), ("z", "c")
    placed = (P(rows, cols, None), P(), P(), P(), P(), P(), P(), P(None, cols, rows))
    return jax.shard_map(body, mesh=torus, in_specs=placed, out_specs=P(rows, cols, None), check_vma=False)
```

```python
import functools
import math

import jax
import jax.numpy as jnp
from jax import lax
from jax.experimental import pallas as pl
from jax.experimental.pallas import tpu as pltpu
from jax.sharding import Mesh
from jax.sharding import PartitionSpec as P

AXES = ("y", "x", "z", "c")
MESH = pl.DeviceIdType.MESH
BF16, F32 = jnp.bfloat16, jnp.float32
NY, NX, NZ, NC = 4, 4, 8, 2
HEADS, DIM, CH = 4, 32, 128
BLK = 48
OWN = BLK // NZ
QRY = NZ * BLK
KEYS = NC * QRY
LANES = 128
CHUNKS = QRY // LANES
EPS = 1e-05
STEP = 128
LOG2E = math.log2(math.e)
Z_ORDER = (4, 3, 5, 2, 6, 1, 7)
NT = (((1,), (1,)), ((), ()))
OFFSETS = (3, 5, 4, 2, 6, 1, 7, 0)
PLACE = tuple(OFFSETS.index(d) for d in range(8))
DONE = ((0, 1), (2, 3, 4), (5, 6, 7))


def dot(a, b):
    return jnp.dot(a, b, preferred_element_type=F32)


def dot_nt(a, b):
    return lax.dot_general(a, b, NT, preferred_element_type=F32)


def kernel(
    x_hbm, gain_hbm, w_query_hbm, w_key_hbm, w_value_hbm, w_gate_hbm, w_out_hbm, pair_bias_hbm, out_hbm,
    gain, w_query, w_key, w_value, w_gate, w_out, pair_bias,
    xbuf, zbias, bias, bias32, keys, values, queries, gates, wq_t, wv_t, wg_t, outbuf, s0, s1, top0, top1, result,
    zs, zr, as_, ar, bs, br, xs, xr, xl, fs, fr, os_, or_, ol, wl,
):
    y, x, z, c = (lax.axis_index(a) for a in AXES)
    at = {"x": x, "y": y}

    def remote(src, dst, send, recv, **where):
        return pltpu.make_async_remote_copy(
            src_ref=src, dst_ref=dst, send_sem=send, recv_sem=recv, device_id=where, device_id_type=MESH
        )

    def wait(ref, sem):
        pltpu.make_async_copy(ref, ref, sem).wait()

    barrier = pltpu.get_barrier_semaphore()
    peers = [{"z": lax.rem(z + k, NZ)} for k in range(1, NZ)]
    peers += [{a: lax.rem(at[a] + k, 4)} for a in "xy" for k in range(1, 4)]
    peers += [{"c": 1 - c}]
    for peer in peers:
        pl.semaphore_signal(barrier, inc=1, device_id=peer, device_id_type=MESH)

    loads = [
        pltpu.make_async_copy(src, dst, wl.at[n])
        for n, (src, dst) in enumerate((
            (pair_bias_hbm, pair_bias), (w_query_hbm, w_query), (w_value_hbm, w_value), (w_gate_hbm, w_gate),
            (w_key_hbm, w_key), (w_out_hbm, w_out), (gain_hbm, gain),
        ))
    ]
    for load in loads:
        load.start()
    own_rows = pltpu.make_async_copy(x_hbm.at[pl.ds(z * OWN, OWN)], xbuf.at[:, 0, PLACE[0]], xl)
    own_rows.start()

    for load in loads:
        load.wait()
    for g in range(2):
        packed = jnp.zeros((BLK, LANES), F32)
        for hh in range(2):
            row = lax.broadcasted_iota(jnp.int32, (BLK, LANES), 0)
            lane = lax.broadcasted_iota(jnp.int32, (BLK, LANES), 1)
            place = jnp.where(lane == row + BLK * hh, 1.0, 0.0).astype(BF16)
            packed = packed + dot(pair_bias[2 * g + hh], place)
        zbias[PLACE[0], g] = packed.astype(BF16)
    for src, dst in ((w_query, wq_t), (w_value, wv_t), (w_gate, wg_t)):
        dst[...] = jnp.transpose(src[...].astype(F32)).astype(BF16)
    values[:, :, 2 * DIM :, :] = jnp.ones((OWN, 2, 16, KEYS), BF16)

    result[...] = jnp.zeros_like(result)

    pl.semaphore_wait(barrier, len(peers))

    for k in Z_ORDER:
        remote(zbias.at[PLACE[0]], zbias.at[PLACE[NZ - k]], zs, zr, z=lax.rem(z + k, NZ)).start()

    def send_row(i, _):
        for k in Z_ORDER:
            t = lax.rem(z + k, NZ)
            remote(x_hbm.at[t * OWN + i], xbuf.at[i, 0, PLACE[NZ - k]], xs, xr.at[i], z=t).start()
        return 0

    lax.fori_loop(0, OWN, send_row, 0)

    wait(zbias.at[pl.ds(0, NZ - 1)], zr)
    o = jnp.where(lax.rem(x, 2) == c, 0, 1)
    x2 = x // 2
    for g in range(2):
        block = zbias[:, g].reshape(QRY, LANES)
        for hh in range(2):
            row = lax.broadcasted_iota(jnp.int32, (BLK, LANES), 0)
            lane = lax.broadcasted_iota(jnp.int32, (BLK, LANES), 1)
            place = jnp.where(lane == row + BLK * hh, 1.0, 0.0).astype(BF16)
            part = dot_nt(place, block).astype(BF16)
            for t in range(CHUNKS):
                bias[t, 2 * g + hh, o, y, x2] = part[:, LANES * t : LANES * (t + 1)]
    for t in range(CHUNKS):
        for half, axis in ((0, "x"), (1, "y")):
            mine = bias.at[t, pl.ds(2 * half, 2), o, y, x2]
            for k in (2, 1, 3):
                there = lax.rem(at[axis] + k, 4)
                remote(mine, mine, as_, ar.at[t, half], **{axis: there}).start()
    for t in range(CHUNKS):
        for half, axis in ((0, "y"), (1, "x")):
            wait(bias.at[t, pl.ds(0, 2), 0, pl.ds(0, 3), 0], ar.at[t, half])
            if half == 0:
                line = bias.at[t, pl.ds(0, 2), :, y]
            else:
                line = bias.at[t, pl.ds(2, 2), o, :, x2]
            for k in (2, 1, 3):
                there = lax.rem(at[axis] + k, 4)
                remote(line, line, bs, br.at[t, half], **{axis: there}).start()

    def normed(i, side):
        v = xbuf[i, side].reshape(QRY, CH).astype(F32)
        v = v - jnp.mean(v, axis=-1, keepdims=True)
        spread = jnp.mean(jnp.square(v), axis=-1, keepdims=True)
        return (v * lax.rsqrt(spread + EPS) * gain[...]).astype(BF16)

    def project(i, side, n):
        cols = pl.ds(side * QRY, QRY)
        keys[i, cols, :] = dot(n, w_key[...]).astype(BF16)
        v = dot_nt(wv_t[...], n).astype(BF16)
        values[i, 0, : 2 * DIM, cols] = v[: 2 * DIM]
        values[i, 1, : 2 * DIM, cols] = v[2 * DIM :]

    own_rows.wait()

    def own_here(i):
        wait(xbuf.at[i, 0, pl.ds(0, NZ - 1)], xr.at[i])
        remote(xbuf.at[i, 0], xbuf.at[i, 1], fs, fr.at[i], c=1 - c).start()

    def own_side(i):
        n = normed(i, 0)
        project(i, 0, n)
        queries[i] = (dot_nt(wq_t[...], n) * (DIM**-0.5 * LOG2E)).astype(BF16)
        gates[i] = jax.nn.sigmoid(dot_nt(wg_t[...], n))

    def other_here(i):
        wait(xbuf.at[i, 1], fr.at[i])

    def other_side(i):
        project(i, 1, normed(i, 1))

    own_here(0)
    own_side(0)

    def prepare(i, _):
        own_here(i + 1)
        other_here(i)
        own_side(i + 1)
        other_side(i)
        return 0

    lax.fori_loop(0, OWN - 1, prepare, 0)
    other_here(OWN - 1)
    other_side(OWN - 1)

    place = []
    for b in range(NZ):
        away = lax.rem(b - z + NZ, NZ)
        place.append(sum(jnp.where(away == d, PLACE[d], 0) for d in range(NZ)))

    for t in range(CHUNKS):
        lanes = slice(LANES * t, LANES * (t + 1))
        for half in range(2):
            wait(bias.at[t, pl.ds(0, 2), :, pl.ds(0, 3)], br.at[t, half])
        for h in range(HEADS):
            for side in range(2):
                for b in range(NZ):
                    rows = pl.ds(pl.multiple_of(side * QRY + BLK * place[b], 16), BLK)
                    bias32[h // 2, rows, LANES * (h % 2) : LANES * (h % 2 + 1)] = (
                        bias[t, h, side, b // 2, b % 2].astype(F32) * LOG2E
                    )

        def scores(i, g, s_ref, top_ref):
            q = queries[i, :, lanes]
            head = lax.broadcasted_iota(jnp.int32, (CH, LANES), 0) // DIM
            rhs = jnp.concatenate([jnp.where(head == 2 * g + hh, q, jnp.zeros_like(q)) for hh in range(2)], axis=1)
            top = None
            for k in range(0, KEYS, STEP):
                s = dot(keys[i, k : k + STEP, :], rhs) + bias32[g, k : k + STEP, :]
                s_ref[k : k + STEP, :] = s
                peak = jnp.max(s.reshape(STEP // 8, 8, 2 * LANES), axis=0)
                top = peak if top is None else jnp.maximum(top, peak)
            top_ref[...] = top

        def weigh(i, g, s_ref, top_ref):
            top = jnp.max(top_ref[...], axis=0, keepdims=True)
            p = [jnp.exp2(s_ref[k : k + STEP, :] - top).astype(BF16) for k in range(0, KEYS, STEP)]
            sums = dot(values[i, g], jnp.concatenate(p, axis=0))
            rows = []
            for hh in range(2):
                side = slice(LANES * hh, LANES * (hh + 1))
                rows.append(sums[DIM * hh : DIM * (hh + 1), side] / sums[2 * DIM : 2 * DIM + 1, side])
            return jnp.concatenate(rows, axis=0)

        scores(0, 0, s0, top0)

        def finish(i):
            gated = jnp.transpose(result[...]).astype(BF16)
            outbuf[i, lanes, :] = dot(gated, w_out[...]).astype(BF16)

        def send(i):
            for b in DONE[t]:
                done, there = outbuf.at[i, pl.ds(BLK * b, BLK)], out_hbm.at[z * OWN + i]
                if OFFSETS[b]:
                    remote(done, there, os_, or_, z=lax.rem(z + OFFSETS[b], NZ)).start()
                else:
                    pltpu.make_async_copy(done, there, ol).start()

        def attend(i, _):
            finish(jnp.maximum(i - 1, 0))
            scores(i, 1, s1, top1)
            first = weigh(i, 0, s0, top0)
            scores(jnp.minimum(i + 1, OWN - 1), 0, s0, top0)
            second = weigh(i, 1, s1, top1)
            result[...] = jnp.concatenate([first, second], axis=0) * gates[i, :, lanes]
            pl.when(i > 0)(lambda: send(i - 1))
            return 0

        lax.fori_loop(0, OWN, attend, 0)
        finish(OWN - 1)
        send(OWN - 1)

    wait(out_hbm.at[pl.ds(0, OWN * (NZ - 1))], or_)
    wait(out_hbm.at[pl.ds(0, OWN * (NZ - 1))], os_)
    wait(out_hbm.at[pl.ds(0, OWN)], ol)
    wait(zbias.at[pl.ds(0, NZ - 1)], zs)
    wait(x_hbm.at[pl.ds(0, OWN * (NZ - 1))], xs)
    wait(xbuf.at[:, 0], fs)
    for t in range(CHUNKS):
        for half in range(2):
            wait(bias.at[t, pl.ds(0, 2), 0, pl.ds(0, 3), 0], as_)
            wait(bias.at[t, pl.ds(0, 2), :, pl.ds(0, 3)], bs)


def body(pair_rep, norm_gain, w_query, w_key, w_value, w_gate, w_out, pair_bias):
    anywhere = pl.BlockSpec(memory_space=pl.ANY)
    dma = pltpu.SemaphoreType.DMA
    return pl.pallas_call(
        kernel,
        out_shape=jax.ShapeDtypeStruct((BLK, BLK, CH), BF16),
        in_specs=[anywhere] * 8,
        out_specs=anywhere,
        scratch_shapes=[
            pltpu.VMEM((1, CH), F32),
            *[pltpu.VMEM((CH, CH), BF16)] * 5,
            pltpu.VMEM((HEADS, BLK, BLK), BF16),
            pltpu.VMEM((OWN, 2, NZ, BLK, CH), BF16),
            pltpu.VMEM((NZ, 2, BLK, LANES), BF16),
            pltpu.VMEM((CHUNKS, HEADS, 2, NY, NX // 2, BLK, LANES), BF16),
            pltpu.VMEM((2, KEYS, 2 * LANES), F32),
            pltpu.VMEM((OWN, KEYS, CH), BF16),
            pltpu.VMEM((OWN, 2, 2 * DIM + 16, KEYS), BF16),
            pltpu.VMEM((OWN, CH, QRY), BF16),
            pltpu.VMEM((OWN, CH, QRY), F32),
            pltpu.VMEM((CH, CH), BF16),
            pltpu.VMEM((CH, CH), BF16),
            pltpu.VMEM((CH, CH), BF16),
            pltpu.VMEM((OWN, QRY, CH), BF16),
            pltpu.VMEM((KEYS, 2 * LANES), F32),
            pltpu.VMEM((KEYS, 2 * LANES), F32),
            pltpu.VMEM((8, 2 * LANES), F32),
            pltpu.VMEM((8, 2 * LANES), F32),
            pltpu.VMEM((CH, LANES), F32),
            dma, dma,
            dma, dma((CHUNKS, 2)),
            dma, dma((CHUNKS, 2)),
            dma, dma((OWN,)), dma,
            dma, dma((OWN,)),
            dma, dma, dma,
            dma((7,)),
        ],
        compiler_params=pltpu.CompilerParams(
            collective_id=0, has_side_effects=True, vmem_limit_bytes=56 * 1024 * 1024
        ),
        name="triangle_attention",
    )(pair_rep, norm_gain.reshape(1, CH), w_query, w_key, w_value, w_gate, w_out, pair_bias)


def solution(mesh):
    torus = Mesh(mesh.devices.reshape(NY, NX, NZ, NC), AXES)
    rows, cols = ("y", "x"), ("z", "c")
    placed = (P(rows, cols, None), P(), P(), P(), P(), P(), P(), P(None, cols, rows))
    return jax.shard_map(body, mesh=torus, in_specs=placed, out_specs=P(rows, cols, None), check_vma=False)
```
